32 devices in a mesh: row: 8 (over z, y), col: 4 (over x, core).
Axes of the slice: x: 2, y: 2, z: 4, core: 2. Of those that a mesh axis runs over, the one named last changes fastest.
Arguments:
- acts: bfloat16 [1024, 3072], P('row', 'col'), may hold values from -6 to 6
- grads: bfloat16 [1024, 3072], P('col', 'row'), may hold values from -0.19921875 to 0.19921875
- next_acts: bfloat16 [256, 3072], P('row', 'col'), may hold values from -6 to 6
- weight: bfloat16 [3072, 3072], P('row', 'col'), may hold values from -0.109375 to 0.109375
- moment: float32 [3072, 3072], P('row', 'col'), may hold values from -6 to 6
- second: float32 [3072, 3072], P('row', 'col'), may hold values from 0.05 to 5
- left_bank: bfloat16 [4, 384, 384], replicated, may hold values from -1 to 1, as said below
- right_bank: bfloat16 [4, 768, 768], P(None, 'row'), may hold values from -1 to 1, as said below
- left_index: int32 [8, 4], P('row', 'col'), may hold values from 0 to 3
- right_index: int32 [8, 4], P('row', 'col'), may hold values from 0 to 3
Outputs:
- update: bfloat16 [3072, 3072], P('row', 'col')
- next_out: bfloat16 [256, 3072], P('col', 'row')
The draws below stay inside these ranges and needn't reach their ends.
Inputs may be any that keep to these rules, and one draw needn't show every extreme that they name: `left_bank`: each basis is an orthogonal matrix rounded to bfloat16. `right_bank`: each basis is an orthogonal matrix rounded to bfloat16.
All inputs are finite; a program needn't handle non-finite values.
Results may differ from the reference program's by a relative error of at most 0.008.
Values may be sent and summed in bfloat16 or wider, within the bound.
A program may use at most 64 MiB of HBM per device.

```python
import math
import jax
import jax.numpy as jnp
from jax import lax

BO = 384
BI = 768
BANK = 4
TOKENS = 1024
NEXT = 256
D_OUT = 3072
D_IN = 3072
N_ROW = 8
N_COL = 4


def orthogonal_bank(key, count, order):
    normals = jax.random.normal(key, (count, order, order), jnp.float32)
    factors = jax.vmap(lambda matrix: jnp.linalg.qr(matrix)[0])(normals)
    return factors.astype(jnp.bfloat16)


def draw_left_bank(key, part):
    return orthogonal_bank(jax.random.fold_in(key, 11), BANK, BO)


def draw_right_bank(key, part):
    return orthogonal_bank(jax.random.fold_in(key, 23), BANK, BI)


def plant(values, stream_key, least, top_value):
    longest = values.shape.index(max(values.shape))
    spots = []
    for shift in (0, 1):
        where = [jax.random.randint(jax.random.fold_in(stream_key, axis), (), 0, length) for axis, length in enumerate(values.shape)]
        where[longest] = (where[longest] + shift) % values.shape[longest]
        spots.append(tuple(where))
    return values.at[spots[0]].set(least).at[spots[1]].set(top_value)


def block_scale(key, dims, split, least, top_value):
    loudness, own = 1.0, jax.random.fold_in(key, 6)
    for axis_at, shards_of in split:
        draws = jnp.exp(jax.random.uniform(jax.random.fold_in(own, axis_at), (shards_of,), jnp.float32, least / len(split), top_value / len(split)))
        loudness = loudness * jnp.repeat(draws, dims[axis_at] // shards_of).reshape([-1 if axis == axis_at else 1 for axis in range(len(dims))])
    return loudness


def normal_values(rng, extent, deviation, reach, cuts=(), dtype=jnp.bfloat16):
    drawn = jax.random.normal(rng, extent, jnp.float32) * deviation
    if len(cuts) > 0:
        drawn = block_scale(rng, extent, cuts, -0.22, 0.18) * drawn
    return jnp.clip(drawn, min=-reach, max=reach).astype(dtype)


def setup_inputs(seed: int = 0) -> dict:
    streams_of = jax.random.split(jax.random.key(seed), 11)
    return {
        "acts": normal_values(streams_of[0], (TOKENS, D_IN), 1.0, 6.0, ((0, 8), (1, 4))),
        "grads": normal_values(streams_of[1], (TOKENS, D_OUT), 0.03, 0.19921875, ((0, 4), (1, 8))),
        "next_acts": normal_values(streams_of[2], (NEXT, D_IN), 1.0, 6.0, ((0, 8), (1, 4))),
        "weight": normal_values(streams_of[3], (D_OUT, D_IN), D_IN ** -0.5, 0.109375, ((0, 8), (1, 4))),
        "moment": normal_values(streams_of[4], (D_OUT, D_IN), 1.0, 6.0, ((0, 8), (1, 4)), jnp.float32),
        "second": jnp.clip(jnp.exp(math.log(5.0) - 4.6051702 * jax.random.uniform(streams_of[5], (D_OUT, D_IN), jnp.float32) ** block_scale(streams_of[5], (D_OUT, D_IN), ((0, 8), (1, 4)), -0.2, 0.2)), 0.05, 5.0),
        "left_bank": draw_left_bank(jax.random.fold_in(streams_of[10], 71), 0),
        "right_bank": draw_right_bank(jax.random.fold_in(streams_of[10], 71), 0),
        "left_index": plant(jax.random.randint(streams_of[8], (N_ROW, N_COL), 0, BANK), jax.random.fold_in(streams_of[8], 1), 0, BANK - 1).astype(jnp.int32),
        "right_index": plant(jax.random.randint(streams_of[9], (N_ROW, N_COL), 0, BANK), jax.random.fold_in(streams_of[9], 1), 0, BANK - 1).astype(jnp.int32),
    }


HIGH = lax.Precision.HIGHEST

def to_blocks(array):
    return array.reshape(N_ROW, BO, N_COL, BI).transpose(0, 2, 1, 3).reshape(N_ROW * N_COL, BO, BI)

def from_blocks(array):
    return array.reshape(N_ROW, N_COL, BO, BI).transpose(0, 2, 1, 3).reshape(N_ROW * BO, N_COL * BI)

def reference(acts, grads, next_acts, weight, moment, second, left_bank, right_bank, left_index, right_index):
    f32 = jnp.float32
    gradient = jnp.dot(grads.astype(f32).T, acts.astype(f32), precision=HIGH).astype(jnp.bfloat16)

    def one_block(items):
        grad_block, weight_block, moment_block, second_block, left_pick, right_pick = items
        left_basis = lax.dynamic_index_in_dim(left_bank, left_pick, 0, keepdims=False).astype(f32)
        right_basis = lax.dynamic_index_in_dim(right_bank, right_pick, 0, keepdims=False).astype(f32)
        half = jnp.dot(left_basis.T, grad_block.astype(f32), precision=HIGH).astype(jnp.bfloat16)
        rotated = jnp.dot(half.astype(f32), right_basis, precision=HIGH)
        new_moment = 0.8 * moment_block + 0.2 * rotated
        new_second = 0.9 * second_block + 0.1 * rotated * rotated
        scaled = (new_moment / (jnp.sqrt(new_second) + 1e-08)).astype(jnp.bfloat16)
        back = jnp.dot(left_basis, scaled.astype(f32), precision=HIGH).astype(jnp.bfloat16)
        update_full = jnp.dot(back.astype(f32), right_basis.T, precision=HIGH)
        new_weight = (weight_block.astype(f32) - 0.001 * update_full).astype(jnp.bfloat16)
        return (update_full.astype(jnp.bfloat16), new_weight)
    updates, weights = lax.map(one_block, (to_blocks(gradient), to_blocks(weight), to_blocks(moment), to_blocks(second), left_index.reshape(-1).astype(jnp.int32), right_index.reshape(-1).astype(jnp.int32)))
    update = from_blocks(updates)
    new_weight = from_blocks(weights)
    next_out = jnp.dot(next_acts.astype(f32), new_weight.astype(f32).T, precision=HIGH).astype(jnp.bfloat16)
    return (update, next_out)
```

```python
import functools

import jax
import jax.numpy as jnp
from jax import lax
from jax.experimental import pallas as pl
from jax.experimental.pallas import tpu as pltpu
from jax.sharding import PartitionSpec as P

F32 = jnp.float32
BF16 = jnp.bfloat16
MESH = pl.DeviceIdType.MESH


def flip(value, bits, size):
    out, place = 0, 1
    while place < size:
        bit = (value // place) % 2
        out = out + place * ((1 - bit) if (bits // place) % 2 else bit)
        place *= 2
    return out


def as_matrix(value):
    cols = value.shape[-1]
    if value.shape[-2] % 16:
        return value.astype(F32).reshape(-1, cols).astype(BF16)
    return value.reshape(-1, cols)


def kernel(
    nz, nc,
    acts, grads, nxt, weight, moment, second, left_bank, right_bank, left_index, right_index,
    update, out,
    afull, gfull, nfull, wbuf, mbuf, sbuf, lbuf, bz, sel, rbuf,
    my_pick, picks, picks_smem, gacc, half, back, part, rsend, rrecv, ubuf, obuf,
    local, a_s, a_r, ay_s, ay_r, n_s, n_r, ny_s, ny_r, b_s, b_r,
    g_s, g_r, p_s, p_r, s_s, s_r, r_s, r_r,
):
    row, col = lax.axis_index("row"), lax.axis_index("col")
    z, y = row // 2, row % 2
    quad, q = col // 4, col % 4
    x, k = q // 2, q % 2
    tok = acts.shape[0]
    gtok = grads.shape[0]
    width = acts.shape[1]
    lanes = width // 2
    slot = y * 4 + q
    my_lanes = pl.ds(pl.multiple_of(x * lanes, 128), lanes)

    def remote(src, dst, ss, rs, device):
        return pltpu.make_async_remote_copy(
            src_ref=src, dst_ref=dst, send_sem=ss, recv_sem=rs,
            device_id=device, device_id_type=MESH,
        )

    z_peers = [(d, flip(z, d, nz)) for d in range(1, nz)]
    plane = [
        (dy * 4 + dq, 2 * z + ((1 - y) if dy else y), quad * 4 + flip(q, dq, 4),
         ((1 - y) if dy else y) * 4 + flip(q, dq, 4))
        for dy in range(2) for dq in range(4) if dy or dq
    ]
    col_peers = [(d, flip(col, d, nc)) for d in range(1, nc)]
    far_cols = [peer for d, peer in col_peers if d >= 4]
    mate = (2 * z + 1 - y, col)

    my_pick[...] = jnp.full(my_pick.shape, right_index[0, 0], jnp.int32)

    loads = [
        (acts, afull.at[z, y]), (nxt, nfull.at[z, y]),
        (grads, gfull.at[pl.ds(pl.multiple_of(col * gtok, gtok), gtok)]),
        (weight, wbuf), (moment, mbuf), (second, sbuf), (left_bank, lbuf),
    ]
    loads = [pltpu.make_async_copy(s, d, local.at[i]) for i, (s, d) in enumerate(loads)]
    own_bank = pltpu.make_async_copy(
        right_bank.at[:, :, my_lanes], bz.at[z // 2], local.at[7]
    )

    @pl.when(z % 2 == k)
    def _():
        own_bank.start()

    for load in loads:
        load.start()

    barrier = pltpu.get_barrier_semaphore()
    friends = [(2 * p + y, col) for _, p in z_peers]
    friends += [(r, c) for _, r, c, _ in plane]
    friends += [(row, c) for c in far_cols]
    for friend in friends:
        pl.semaphore_signal(barrier, inc=1, device_id=friend, device_id_type=MESH)
    pl.semaphore_wait(barrier, len(friends))

    sends = []

    def go(copy):
        copy.start()
        sends.append(copy)

    for e, r, c, _ in plane:
        go(remote(my_pick, picks.at[slot], p_s.at[e], p_r.at[slot], (r, c)))
    bank_sends = [
        remote(right_bank.at[:, :, my_lanes], bz.at[z // 2], b_s.at[d], b_r.at[z // 2],
               (2 * p + y, col))
        for d, p in z_peers
    ]

    @pl.when(z % 2 == k)
    def _():
        for copy in bank_sends:
            copy.start()

    go(remote(acts, afull.at[z, y], ay_s.at[0], ay_r.at[z], mate))
    for d, p in z_peers:
        go(remote(acts, afull.at[z, y], a_s.at[d], a_r.at[z], (2 * p + y, col)))
    for d, c in col_peers:
        go(remote(grads, gfull.at[pl.ds(pl.multiple_of(col * gtok, gtok), gtok)],
                  g_s.at[d], g_r.at[col], (row, c)))
    for d, p in z_peers:
        go(remote(nxt, nfull.at[z, y], n_s.at[d], n_r.at[z], (2 * p + y, col)))

    picks[slot] = my_pick[...]
    for e, r, c, s in plane:
        remote(my_pick, picks.at[s], p_s.at[e], p_r.at[s], (r, c)).wait_recv()
    to_smem = pltpu.make_async_copy(picks, picks_smem, local.at[8])
    to_smem.start()
    to_smem.wait()

    for d in range(nz):
        zs = flip(z, d, nz) if d else z

        @pl.when(zs % 2 == k)
        def _(d=d, zs=zs):
            if d == 0:
                own_bank.wait()
            else:
                remote(right_bank.at[:, :, my_lanes], bz.at[zs // 2], b_s.at[d],
                       b_r.at[zs // 2], (2 * zs + y, col)).wait_recv()

    sel[0] = bz[:, picks_smem[slot, 0, 0]]
    for e, r, c, s in plane:
        sel[e] = bz[:, picks_smem[s, 0, 0]]
    own_sel = pltpu.make_async_copy(sel.at[0], rbuf.at[:, k, y, :, my_lanes], local.at[9])
    own_sel.start()
    for e, r, c, _ in plane:
        go(remote(sel.at[e], rbuf.at[:, k, y, :, my_lanes], s_s.at[e], s_r.at[slot], (r, c)))

    for d, p in z_peers:
        remote(acts, afull.at[p, y], a_s.at[d], a_r.at[p], mate).wait_recv()
        go(remote(afull.at[p, y], afull.at[p, y], ay_s.at[d], ay_r.at[p], mate))
    go(remote(nxt, nfull.at[z, y], ny_s.at[0], ny_r.at[z], mate))
    for d, p in z_peers:
        remote(nxt, nfull.at[p, y], n_s.at[d], n_r.at[p], mate).wait_recv()
        go(remote(nfull.at[p, y], nfull.at[p, y], ny_s.at[d], ny_r.at[p], mate))

    for i in (0, 2):
        loads[i].wait()
    for d, c in col_peers:
        remote(grads, gfull.at[pl.ds(pl.multiple_of(c * gtok, gtok), gtok)],
               g_s.at[d], g_r.at[c], (row, c)).wait_recv()

    for d in range(nz):
        zs = flip(z, d, nz) if d else z
        remote(acts, afull.at[zs, 1 - y], ay_s.at[0], ay_r.at[zs], mate).wait_recv()
        term = lax.dot_general(
            gfull[pl.ds(pl.multiple_of(zs * 2 * tok, 2 * tok), 2 * tok)],
            afull[zs].reshape(2 * tok, width),
            (((0,), (0,)), ((), ())), preferred_element_type=F32,
        )
        if d == 0:
            gacc[...] = term
        else:
            gacc[...] += term

    loads[6].wait()
    left = lbuf[left_index[0, 0]]
    half[...] = lax.dot_general(
        left, gacc[...].astype(BF16), (((0,), (0,)), ((), ())), preferred_element_type=F32
    ).astype(BF16)

    own_sel.wait()
    for e, r, c, s in plane:
        ys, qs = s // 4, s % 4
        src_lanes = pl.ds(pl.multiple_of((qs // 2) * lanes, 128), lanes)
        remote(sel.at[e], rbuf.at[:, qs % 2, ys, :, src_lanes], s_s.at[e], s_r.at[s],
               (r, c)).wait_recv()
    for i in (3, 4, 5):
        loads[i].wait()
    step = 256 if width % 256 == 0 else width
    right = as_matrix(rbuf[...])
    for n in range(0, width, step):
        cut = slice(n, n + step)
        rotated = jnp.dot(half[...], right[:, cut], preferred_element_type=F32)
        new_moment = 0.8 * mbuf[:, cut] + 0.2 * rotated
        new_second = 0.9 * sbuf[:, cut] + 0.1 * rotated * rotated
        scaled = (new_moment / (jnp.sqrt(new_second) + 1e-08)).astype(BF16)
        back[:, cut] = jnp.dot(left, scaled, preferred_element_type=F32).astype(BF16)

    loads[1].wait()
    for d in range(nz):
        zs = flip(z, d, nz) if d else z
        remote(nxt, nfull.at[zs, 1 - y], ny_s.at[0], ny_r.at[zs], mate).wait_recv()
    rows = nfull.shape[0] * nfull.shape[1] * nfull.shape[2]
    for n in range(0, width, step):
        cut = slice(n, n + step)
        full = lax.dot_general(
            back[...], right[cut, :], (((1,), (1,)), ((), ())), preferred_element_type=F32
        )
        ubuf[:, cut] = full.astype(BF16)
        new_weight = (wbuf[:, cut].astype(F32) - 0.001 * full).astype(BF16)
        term = lax.dot_general(
            nfull[:, :, :, cut].reshape(rows, step), new_weight,
            (((1,), (1,)), ((), ())), preferred_element_type=F32,
        )
        if n == 0:
            part[...] = term
        else:
            part[...] += term
    put = pltpu.make_async_copy(ubuf, update, local.at[3])
    put.start()

    share = rows // nc
    rsend[...] = part[...].astype(BF16).reshape(nc, share, part.shape[1])
    for d, c in col_peers:
        go(remote(rsend.at[c], rrecv.at[d - 1], r_s.at[d], r_r.at[d], (row, c)))
    total = part[pl.ds(pl.multiple_of(col * share, share), share)]
    for d, c in col_peers:
        remote(rsend.at[c], rrecv.at[d - 1], r_s.at[d], r_r.at[d], (row, c)).wait_recv()
        total = total + rrecv[d - 1].astype(F32)
    obuf[...] = total.astype(BF16)
    put_out = pltpu.make_async_copy(obuf, out, local.at[4])
    put_out.start()

    for copy in sends:
        copy.wait_send()

    @pl.when(z % 2 == k)
    def _():
        for copy in bank_sends:
            copy.wait_send()

    put.wait()
    put_out.wait()


def per_device(
    acts, grads, next_acts, weight, moment, second, left_bank, right_bank, left_index, right_index,
    *, nr, nc,
):
    nz = nr // 2
    tok, width = acts.shape
    gtok, bo = grads.shape
    ntok = next_acts.shape[0]
    bank, rrows, _ = right_bank.shape
    lanes = width // 2
    share = nr * ntok // nc
    dma = pltpu.SemaphoreType.DMA
    anyspace = pl.BlockSpec(memory_space=pl.ANY)
    smem = pl.BlockSpec(memory_space=pltpu.SMEM)
    return pl.pallas_call(
        functools.partial(kernel, nz, nc),
        out_shape=(
            jax.ShapeDtypeStruct(weight.shape, BF16),
            jax.ShapeDtypeStruct((share, bo), BF16),
        ),
        in_specs=[anyspace] * 8 + [smem] * 2,
        out_specs=(anyspace, anyspace),
        scratch_shapes=[
            pltpu.VMEM((nz, 2, tok, width), BF16),
            pltpu.VMEM((nc * gtok, bo), BF16),
            pltpu.VMEM((nz, 2, ntok, width), BF16),
            pltpu.VMEM(weight.shape, BF16),
            pltpu.VMEM(weight.shape, F32),
            pltpu.VMEM(weight.shape, F32),
            pltpu.VMEM(left_bank.shape, BF16),
            pltpu.VMEM((nz // 2, bank, rrows, lanes), BF16),
            pltpu.VMEM((8, nz // 2, rrows, lanes), BF16),
            pltpu.VMEM((nz // 2, 2, 2, rrows, width), BF16),
            pltpu.VMEM((8, 128), jnp.int32),
            pltpu.VMEM((8, 8, 128), jnp.int32),
            pltpu.SMEM((8, 8, 128), jnp.int32),
            pltpu.VMEM(weight.shape, F32),
            pltpu.VMEM(weight.shape, BF16),
            pltpu.VMEM(weight.shape, BF16),
            pltpu.VMEM((nr * ntok, bo), F32),
            pltpu.VMEM((nc, share, bo), BF16),
            pltpu.VMEM((nc - 1, share, bo), BF16),
            pltpu.VMEM(weight.shape, BF16),
            pltpu.VMEM((share, bo), BF16),
            dma((10,)),
            dma((nz,)), dma((nz,)), dma((nz,)), dma((nz,)),
            dma((nz,)), dma((nz,)), dma((nz,)), dma((nz,)),
            dma((nz,)), dma((nz // 2,)),
            dma((nc,)), dma((nc,)),
            dma((8,)), dma((8,)), dma((8,)), dma((8,)),
            dma((nc,)), dma((nc,)),
        ],
        compiler_params=pltpu.CompilerParams(
            collective_id=0, has_side_effects=True, vmem_limit_bytes=60 * 2**20,
        ),
    )(acts, grads, next_acts, weight, moment, second, left_bank, right_bank, left_index,
      right_index)


def solution(mesh):
    nr, nc = mesh.shape["row"], mesh.shape["col"]
    return jax.shard_map(
        functools.partial(per_device, nr=nr, nc=nc),
        mesh=mesh,
        in_specs=(
            P("row", "col"), P("col", "row"), P("row", "col"), P("row", "col"),
            P("row", "col"), P("row", "col"), P(), P(None, "row", None),
            P("row", "col"), P("row", "col"),
        ),
        out_specs=(P("row", "col"), P("col", "row")),
        check_vma=False,
    )
```

```python
import functools

import jax
import jax.numpy as jnp
from jax import lax
from jax.experimental import pallas as pl
from jax.experimental.pallas import tpu as pltpu
from jax.sharding import PartitionSpec as P

F32 = jnp.float32
BF16 = jnp.bfloat16
MESH = pl.DeviceIdType.MESH


def flip(value, bits, size):
    out, place = 0, 1
    while place < size:
        bit = (value // place) % 2
        out = out + place * ((1 - bit) if (bits // place) % 2 else bit)
        place *= 2
    return out


def as_matrix(value):
    cols = value.shape[-1]
    if value.shape[-2] % 16:
        return value.astype(F32).reshape(-1, cols).astype(BF16)
    return value.reshape(-1, cols)


def kernel(
    nz, nc,
    acts, grads, nxt, weight, moment, second, left_bank, right_bank, left_index, right_index,
    update, out,
    afull, gfull, nfull, wbuf, mbuf, sbuf, lbuf, bz, sel, rbuf,
    my_pick, picks, picks_smem, gacc, half, back, part, rsend, rrecv, ubuf, obuf,
    local, a_s, a_r, ay_s, ay_r, n_s, n_r, ny_s, ny_r, b_s, b_r,
    g_s, g_r, p_s, p_r, s_s, s_r, r_s, r_r,
):
    row, col = lax.axis_index("row"), lax.axis_index("col")
    z, y = row // 2, row % 2
    quad, q = col // 4, col % 4
    x, k = q // 2, q % 2
    tok = acts.shape[0]
    gtok = grads.shape[0]
    width = acts.shape[1]
    lanes = width // 2
    slot = y * 4 + q
    my_lanes = pl.ds(pl.multiple_of(x * lanes, 128), lanes)

    def remote(src, dst, ss, rs, device):
        return pltpu.make_async_remote_copy(
            src_ref=src, dst_ref=dst, send_sem=ss, recv_sem=rs,
            device_id=device, device_id_type=MESH,
        )

    z_peers = [(d, flip(z, d, nz)) for d in range(1, nz)]
    plane = [
        (dy * 4 + dq, 2 * z + ((1 - y) if dy else y), quad * 4 + flip(q, dq, 4),
         ((1 - y) if dy else y) * 4 + flip(q, dq, 4))
        for dy in range(2) for dq in range(4) if dy or dq
    ]
    col_peers = [(d, flip(col, d, nc)) for d in range(1, nc)]
    far_cols = [peer for d, peer in col_peers if d >= 4]
    mate = (2 * z + 1 - y, col)

    my_pick[...] = jnp.full(my_pick.shape, right_index[0, 0], jnp.int32)

    loads = [
        (acts, afull.at[z, y]), (nxt, nfull.at[z, y]),
        (grads, gfull.at[pl.ds(pl.multiple_of(col * gtok, gtok), gtok)]),
        (weight, wbuf), (moment, mbuf), (second, sbuf), (left_bank, lbuf),
    ]
    loads = [pltpu.make_async_copy(s, d, local.at[i]) for i, (s, d) in enumerate(loads)]
    own_bank = pltpu.make_async_copy(
        right_bank.at[:, :, my_lanes], bz.at[z // 2], local.at[7]
    )

    @pl.when(z % 2 == k)
    def _():
        own_bank.start()

    for load in loads:
        load.start()

    barrier = pltpu.get_barrier_semaphore()
    friends = [(2 * p + y, col) for _, p in z_peers]
    friends += [(r, c) for _, r, c, _ in plane]
    friends += [(row, c) for c in far_cols]
    for friend in friends:
        pl.semaphore_signal(barrier, inc=1, device_id=friend, device_id_type=MESH)
    pl.semaphore_wait(barrier, len(friends))

    sends, guards = [], []

    def go(copy):
        copy.start()
        sends.append(copy)

    for e, r, c, _ in plane:
        go(remote(my_pick, picks.at[slot], p_s.at[e], p_r.at[slot], (r, c)))
    bank_src = right_bank.at[:, :, my_lanes]
    up, down = (2 * (z + 1) + y, col), (2 * (z - 1) + y, col)
    has_up, has_down = z < nz - 1, z > 0

    def guarded(cond, copy):
        @pl.when(cond)
        def _():
            copy.start()

        guards.append((cond, copy))

    def bank_copy(src, zs, ss, device):
        return remote(src, bz.at[zs // 2], ss, b_r.at[zs // 2], device)

    def both_ways(make, mine):
        guarded(has_up & mine, make(0, up))
        guarded(has_down & mine, make(1, down))

    yes = z >= 0
    go(remote(nxt, nfull.at[z, y], ny_s.at[0], ny_r.at[0], mate))
    both_ways(lambda i, to: bank_copy(bank_src, z, b_s.at[nz + i], to), z % 2 == k)
    both_ways(lambda i, to: remote(acts, afull.at[z, y], a_s.at[nz + i], a_r.at[z], to), yes)
    go(remote(acts, afull.at[z, y], ay_s.at[z], ay_r.at[z], mate))
    for d, c in col_peers:
        go(remote(grads, gfull.at[pl.ds(pl.multiple_of(col * gtok, gtok), gtok)],
                  g_s.at[d], g_r.at[col], (row, c)))
    loads[1].wait()
    remote(nxt, nfull.at[z, 1 - y], ny_s.at[0], ny_r.at[0], mate).wait_recv()
    both_ways(lambda i, to: remote(nfull.at[z], nfull.at[z], n_s.at[nz + i], n_r.at[z], to), yes)

    picks[slot] = my_pick[...]
    for e, r, c, s in plane:
        remote(my_pick, picks.at[s], p_s.at[e], p_r.at[s], (r, c)).wait_recv()
    to_smem = pltpu.make_async_copy(picks, picks_smem, local.at[8])
    to_smem.start()
    to_smem.wait()

    @pl.when(z % 2 == k)
    def _():
        own_bank.wait()

    def take(valid, copy):
        @pl.when(valid)
        def _():
            copy.wait_recv()

    def forward(hop, what):
        for zs, valid, on, to in ((z - hop, z >= hop, has_up, up),
                                  (z + hop, z + hop < nz, has_down, down)):
            zs = lax.rem(zs + nz, nz)
            if what == "bank":
                valid = valid & (zs % 2 == k)
                copy = bank_copy(bz.at[zs // 2], zs, b_s.at[zs], to)
            elif what == "acts":
                copy = remote(afull.at[zs, y], afull.at[zs, y], a_s.at[zs], a_r.at[zs], to)
            else:
                copy = remote(nfull.at[zs], nfull.at[zs], n_s.at[zs], n_r.at[zs], to)
            take(valid, copy)
            if hop < nz - 1:
                guarded(valid & on, copy)
            if what == "acts":
                guarded(valid, remote(afull.at[zs, y], afull.at[zs, y], ay_s.at[zs],
                                      ay_r.at[zs], mate))

    for hop in range(1, nz):
        forward(hop, "bank")
        if hop < nz - 1:
            forward(hop, "acts")
    sel[0] = bz[:, picks_smem[slot, 0, 0]]
    for e, r, c, s in plane:
        sel[e] = bz[:, picks_smem[s, 0, 0]]
    own_sel = pltpu.make_async_copy(sel.at[0], rbuf.at[:, k, y, :, my_lanes], local.at[9])
    own_sel.start()
    for e, r, c, _ in plane:
        go(remote(sel.at[e], rbuf.at[:, k, y, :, my_lanes], s_s.at[e], s_r.at[slot], (r, c)))


    forward(nz - 1, "acts")
    for hop in range(1, nz):
        forward(hop, "next")

    for i in (0, 2):
        loads[i].wait()
    for d, c in col_peers:
        remote(grads, gfull.at[pl.ds(pl.multiple_of(c * gtok, gtok), gtok)],
               g_s.at[d], g_r.at[c], (row, c)).wait_recv()

    for d in range(nz):
        zs = flip(z, d, nz) if d else z
        remote(acts, afull.at[zs, 1 - y], ay_s.at[0], ay_r.at[zs], mate).wait_recv()
        term = lax.dot_general(
            gfull[pl.ds(pl.multiple_of(zs * 2 * tok, 2 * tok), 2 * tok)],
            afull[zs].reshape(2 * tok, width),
            (((0,), (0,)), ((), ())), preferred_element_type=F32,
        )
        if d == 0:
            gacc[...] = term
        else:
            gacc[...] += term

    loads[6].wait()
    left = lbuf[left_index[0, 0]]
    half[...] = lax.dot_general(
        left, gacc[...].astype(BF16), (((0,), (0,)), ((), ())), preferred_element_type=F32
    ).astype(BF16)

    own_sel.wait()
    for e, r, c, s in plane:
        ys, qs = s // 4, s % 4
        src_lanes = pl.ds(pl.multiple_of((qs // 2) * lanes, 128), lanes)
        remote(sel.at[e], rbuf.at[:, qs % 2, ys, :, src_lanes], s_s.at[e], s_r.at[s],
               (r, c)).wait_recv()
    for i in (3, 4, 5):
        loads[i].wait()
    step = 256 if width % 256 == 0 else width
    right = as_matrix(rbuf[...])
    for n in range(0, width, step):
        cut = slice(n, n + step)
        rotated = jnp.dot(half[...], right[:, cut], preferred_element_type=F32)
        new_moment = 0.8 * mbuf[:, cut] + 0.2 * rotated
        new_second = 0.9 * sbuf[:, cut] + 0.1 * rotated * rotated
        scaled = (new_moment / (jnp.sqrt(new_second) + 1e-08)).astype(BF16)
        back[:, cut] = jnp.dot(left, scaled, preferred_element_type=F32).astype(BF16)

    rows = nfull.shape[0] * nfull.shape[1] * nfull.shape[2]
    for n in range(0, width, step):
        cut = slice(n, n + step)
        full = lax.dot_general(
            back[...], right[cut, :], (((1,), (1,)), ((), ())), preferred_element_type=F32
        )
        ubuf[:, cut] = full.astype(BF16)
        new_weight = (wbuf[:, cut].astype(F32) - 0.001 * full).astype(BF16)
        term = lax.dot_general(
            nfull[:, :, :, cut].reshape(rows, step), new_weight,
            (((1,), (1,)), ((), ())), preferred_element_type=F32,
        )
        if n == 0:
            part[...] = term
        else:
            part[...] += term
    put = pltpu.make_async_copy(ubuf, update, local.at[3])
    put.start()

    share = rows // nc
    rsend[...] = part[...].astype(BF16).reshape(nc, share, part.shape[1])
    for d, c in col_peers:
        go(remote(rsend.at[c], rrecv.at[d - 1], r_s.at[d], r_r.at[d], (row, c)))
    total = part[pl.ds(pl.multiple_of(col * share, share), share)]
    for d, c in col_peers:
        remote(rsend.at[c], rrecv.at[d - 1], r_s.at[d], r_r.at[d], (row, c)).wait_recv()
        total = total + rrecv[d - 1].astype(F32)
    obuf[...] = total.astype(BF16)
    put_out = pltpu.make_async_copy(obuf, out, local.at[4])
    put_out.start()

    for copy in sends:
        copy.wait_send()

    for cond, copy in guards:
        @pl.when(cond)
        def _(copy=copy):
            copy.wait_send()

    put.wait()
    put_out.wait()


def per_device(
    acts, grads, next_acts, weight, moment, second, left_bank, right_bank, left_index, right_index,
    *, nr, nc,
):
    nz = nr // 2
    tok, width = acts.shape
    gtok, bo = grads.shape
    ntok = next_acts.shape[0]
    bank, rrows, _ = right_bank.shape
    lanes = width // 2
    share = nr * ntok // nc
    dma = pltpu.SemaphoreType.DMA
    anyspace = pl.BlockSpec(memory_space=pl.ANY)
    smem = pl.BlockSpec(memory_space=pltpu.SMEM)
    return pl.pallas_call(
        functools.partial(kernel, nz, nc),
        out_shape=(
            jax.ShapeDtypeStruct(weight.shape, BF16),
            jax.ShapeDtypeStruct((share, bo), BF16),
        ),
        in_specs=[anyspace] * 8 + [smem] * 2,
        out_specs=(anyspace, anyspace),
        scratch_shapes=[
            pltpu.VMEM((nz, 2, tok, width), BF16),
            pltpu.VMEM((nc * gtok, bo), BF16),
            pltpu.VMEM((nz, 2, ntok, width), BF16),
            pltpu.VMEM(weight.shape, BF16),
            pltpu.VMEM(weight.shape, F32),
            pltpu.VMEM(weight.shape, F32),
            pltpu.VMEM(left_bank.shape, BF16),
            pltpu.VMEM((nz // 2, bank, rrows, lanes), BF16),
            pltpu.VMEM((8, nz // 2, rrows, lanes), BF16),
            pltpu.VMEM((nz // 2, 2, 2, rrows, width), BF16),
            pltpu.VMEM((8, 128), jnp.int32),
            pltpu.VMEM((8, 8, 128), jnp.int32),
            pltpu.SMEM((8, 8, 128), jnp.int32),
            pltpu.VMEM(weight.shape, F32),
            pltpu.VMEM(weight.shape, BF16),
            pltpu.VMEM(weight.shape, BF16),
            pltpu.VMEM((nr * ntok, bo), F32),
            pltpu.VMEM((nc, share, bo), BF16),
            pltpu.VMEM((nc - 1, share, bo), BF16),
            pltpu.VMEM(weight.shape, BF16),
            pltpu.VMEM((share, bo), BF16),
            dma((10,)),
            dma((nz + 2,)), dma((nz,)), dma((nz,)), dma((nz,)),
            dma((nz + 2,)), dma((nz,)), dma((1,)), dma((1,)),
            dma((nz + 2,)), dma((nz // 2,)),
            dma((nc,)), dma((nc,)),
            dma((8,)), dma((8,)), dma((8,)), dma((8,)),
            dma((nc,)), dma((nc,)),
        ],
        compiler_params=pltpu.CompilerParams(
            collective_id=0, has_side_effects=True, vmem_limit_bytes=60 * 2**20,
        ),
    )(acts, grads, next_acts, weight, moment, second, left_bank, right_bank, left_index,
      right_index)


def solution(mesh):
    nr, nc = mesh.shape["row"], mesh.shape["col"]
    return jax.shard_map(
        functools.partial(per_device, nr=nr, nc=nc),
        mesh=mesh,
        in_specs=(
            P("row", "col"), P("col", "row"), P("row", "col"), P("row", "col"),
            P("row", "col"), P("row", "col"), P(), P(None, "row", None),
            P("row", "col"), P("row", "col"),
        ),
        out_specs=(P("row", "col"), P("col", "row")),
        check_vma=False,
    )
```

```python
import functools

import jax
import jax.numpy as jnp
from jax import lax
from jax.experimental import pallas as pl
from jax.experimental.pallas import tpu as pltpu
from jax.sharding import PartitionSpec as P

F32 = jnp.float32
BF16 = jnp.bfloat16
MESH = pl.DeviceIdType.MESH


def flip(value, bits, size):
    out, place = 0, 1
    while place < size:
        bit = (value // place) % 2
        out = out + place * ((1 - bit) if (bits // place) % 2 else bit)
        place *= 2
    return out


def as_matrix(value):
    cols = value.shape[-1]
    if value.shape[-2] % 16:
        return value.astype(F32).reshape(-1, cols).astype(BF16)
    return value.reshape(-1, cols)


def kernel(
    nz, nc,
    acts, grads, nxt, weight, moment, second, left_bank, right_bank, left_index, right_index,
    update, out,
    afull, gfull, nfull, wbuf, mbuf, sbuf, lbuf, bz, sel, rbuf,
    my_pick, picks, picks_smem, gacc, half, back, part, rsend, rrecv, ubuf, obuf,
    local, a_s, a_r, ay_s, ay_r, n_s, n_r, ny_s, ny_r, b_s, b_r,
    g_s, g_r, p_s, p_r, s_s, s_r, own_s, r_s, r_r,
):
    row, col = lax.axis_index("row"), lax.axis_index("col")
    z, y = row // 2, row % 2
    quad, q = col // 4, col % 4
    x, k = q // 2, q % 2
    tok = acts.shape[0]
    gtok = grads.shape[0]
    width = acts.shape[1]
    lanes = width // 2
    slot = y * 4 + q
    my_lanes = pl.ds(pl.multiple_of(x * lanes, 128), lanes)

    def remote(src, dst, ss, rs, device):
        return pltpu.make_async_remote_copy(
            src_ref=src, dst_ref=dst, send_sem=ss, recv_sem=rs,
            device_id=device, device_id_type=MESH,
        )

    z_peers = [(d, flip(z, d, nz)) for d in range(1, nz)]
    plane = [
        (dy * 4 + dq, 2 * z + ((1 - y) if dy else y), quad * 4 + flip(q, dq, 4),
         ((1 - y) if dy else y) * 4 + flip(q, dq, 4))
        for dy in range(2) for dq in range(4) if dy or dq
    ]
    col_peers = [(d, flip(col, d, nc)) for d in range(1, nc)]
    far_cols = [peer for d, peer in col_peers if d >= 4]
    mate = (2 * z + 1 - y, col)

    my_pick[...] = jnp.full(my_pick.shape, right_index[0, 0], jnp.int32)

    loads = [
        (acts, afull.at[z, y]), (nxt, nfull.at[z, y]),
        (grads, gfull.at[pl.ds(pl.multiple_of(col * gtok, gtok), gtok)]),
        (weight, wbuf), (moment, mbuf), (second, sbuf), (left_bank, lbuf),
    ]
    loads = [pltpu.make_async_copy(s, d, local.at[i]) for i, (s, d) in enumerate(loads)]
    own_bank = pltpu.make_async_copy(
        right_bank.at[:, :, my_lanes], bz.at[z // 2], local.at[7]
    )

    @pl.when(z % 2 == k)
    def _():
        own_bank.start()

    for load in loads:
        load.start()

    barrier = pltpu.get_barrier_semaphore()
    friends = [(2 * p + y, col) for _, p in z_peers]
    friends += [(r, c) for _, r, c, _ in plane]
    friends += [(row, c) for c in far_cols]
    for friend in friends:
        pl.semaphore_signal(barrier, inc=1, device_id=friend, device_id_type=MESH)
    pl.semaphore_wait(barrier, len(friends))

    sends, guards, handed = [], [], []

    def go(copy):
        copy.start()
        sends.append(copy)

    for e, r, c, _ in plane:
        go(remote(my_pick, picks.at[slot], p_s.at[e], p_r.at[slot], (r, c)))
    bank_src = right_bank.at[:, :, my_lanes]
    up, down = (2 * (z + 1) + y, col), (2 * (z - 1) + y, col)
    has_up, has_down = z < nz - 1, z > 0

    def guarded(cond, copy):
        @pl.when(cond)
        def _():
            copy.start()

        guards.append((cond, copy))

    def bank_copy(src, zs, ss, device):
        return remote(src, bz.at[zs // 2], ss, b_r.at[zs // 2], device)

    def both_ways(make, mine):
        guarded(has_up & mine, make(0, up))
        guarded(has_down & mine, make(1, down))

    yes = z >= 0
    go(remote(nxt, nfull.at[z, y], ny_s.at[0], ny_r.at[0], mate))
    both_ways(lambda i, to: bank_copy(bank_src, z, b_s.at[nz + i], to), z % 2 == k)
    both_ways(lambda i, to: remote(acts, afull.at[z, y], a_s.at[nz + i], a_r.at[z], to), yes)
    go(remote(acts, afull.at[z, y], ay_s.at[z], ay_r.at[z], mate))
    for d, c in col_peers:
        go(remote(grads, gfull.at[pl.ds(pl.multiple_of(col * gtok, gtok), gtok)],
                  g_s.at[d], g_r.at[col], (row, c)))
    loads[1].wait()
    remote(nxt, nfull.at[z, 1 - y], ny_s.at[0], ny_r.at[0], mate).wait_recv()
    both_ways(lambda i, to: remote(nfull.at[z], nfull.at[z], n_s.at[nz + i], n_r.at[z], to), yes)

    picks[slot] = my_pick[...]
    for e, r, c, s in plane:
        remote(my_pick, picks.at[s], p_s.at[e], p_r.at[s], (r, c)).wait_recv()
    to_smem = pltpu.make_async_copy(picks, picks_smem, local.at[8])
    to_smem.start()
    to_smem.wait()

    def place(zs, slot_from):
        ys, qs = slot_from // 4, slot_from % 4
        at = pl.ds(pl.multiple_of((qs // 2) * lanes, 128), lanes)
        return rbuf.at[zs // 2, qs % 2, ys, :, at]

    def plane_copy(zs, e, s, device):
        i = zs // 2
        return remote(sel.at[i, e], place(zs, s), s_s.at[i, e], s_r.at[i, s], device)

    def own_copy(zs):
        return pltpu.make_async_copy(sel.at[zs // 2, 0], place(zs, slot), own_s.at[zs // 2])

    def hand_out(zs, valid):
        @pl.when(valid)
        def _():
            for e, s in [(0, slot)] + [(e, s) for e, _, _, s in plane]:
                pick = picks_smem[s, 0, 0]
                piece = bz[zs // 2, 0]
                for b in range(1, bz.shape[1]):
                    piece = jnp.where(pick == b, bz[zs // 2, b], piece)
                sel[zs // 2, e] = piece
            own_copy(zs).start()
            for e, r, c, _ in plane:
                plane_copy(zs, e, slot, (r, c)).start()

        handed.append((zs, valid))

    @pl.when(z % 2 == k)
    def _():
        own_bank.wait()

    hand_out(z, z % 2 == k)

    def take(valid, copy):
        @pl.when(valid)
        def _():
            copy.wait_recv()

    def forward(hop, what):
        for zs, valid, on, to in ((z - hop, z >= hop, has_up, up),
                                  (z + hop, z + hop < nz, has_down, down)):
            zs = lax.rem(zs + nz, nz)
            if what == "bank":
                valid = valid & (zs % 2 == k)
                copy = bank_copy(bz.at[zs // 2], zs, b_s.at[zs], to)
            elif what == "acts":
                copy = remote(afull.at[zs, y], afull.at[zs, y], a_s.at[zs], a_r.at[zs], to)
            else:
                copy = remote(nfull.at[zs], nfull.at[zs], n_s.at[zs], n_r.at[zs], to)
            take(valid, copy)
            if hop < nz - 1:
                guarded(valid & on, copy)
            if what == "bank":
                hand_out(zs, valid)
            if what == "acts":
                guarded(valid, remote(afull.at[zs, y], afull.at[zs, y], ay_s.at[zs],
                                      ay_r.at[zs], mate))

    for hop in range(1, nz):
        forward(hop, "bank")
        if hop < nz - 1:
            forward(hop, "acts")
    forward(nz - 1, "acts")
    for hop in range(1, nz):
        forward(hop, "next")

    for i in (0, 2):
        loads[i].wait()
    for d, c in col_peers:
        remote(grads, gfull.at[pl.ds(pl.multiple_of(c * gtok, gtok), gtok)],
               g_s.at[d], g_r.at[c], (row, c)).wait_recv()

    for d in range(nz):
        zs = flip(z, d, nz) if d else z
        remote(acts, afull.at[zs, 1 - y], ay_s.at[0], ay_r.at[zs], mate).wait_recv()
        term = lax.dot_general(
            gfull[pl.ds(pl.multiple_of(zs * 2 * tok, 2 * tok), 2 * tok)],
            afull[zs].reshape(2 * tok, width),
            (((0,), (0,)), ((), ())), preferred_element_type=F32,
        )
        if d == 0:
            gacc[...] = term
        else:
            gacc[...] += term

    loads[6].wait()
    left = lbuf[left_index[0, 0]]
    half[...] = lax.dot_general(
        left, gacc[...].astype(BF16), (((0,), (0,)), ((), ())), preferred_element_type=F32
    ).astype(BF16)

    for i in range(nz // 2):
        for e, r, c, s in plane:
            plane_copy(2 * i, e, s, (r, c)).wait_recv()
    for zs, valid in handed:
        @pl.when(valid)
        def _(zs=zs):
            own_copy(zs).wait()

    for i in (3, 4, 5):
        loads[i].wait()
    step = 256 if width % 256 == 0 else width
    right = as_matrix(rbuf[...])
    for n in range(0, width, step):
        cut = slice(n, n + step)
        rotated = jnp.dot(half[...], right[:, cut], preferred_element_type=F32)
        new_moment = 0.8 * mbuf[:, cut] + 0.2 * rotated
        new_second = 0.9 * sbuf[:, cut] + 0.1 * rotated * rotated
        scaled = (new_moment / (jnp.sqrt(new_second) + 1e-08)).astype(BF16)
        back[:, cut] = jnp.dot(left, scaled, preferred_element_type=F32).astype(BF16)

    rows = nfull.shape[0] * nfull.shape[1] * nfull.shape[2]
    for n in range(0, width, step):
        cut = slice(n, n + step)
        full = lax.dot_general(
            back[...], right[cut, :], (((1,), (1,)), ((), ())), preferred_element_type=F32
        )
        ubuf[:, cut] = full.astype(BF16)
        new_weight = (wbuf[:, cut].astype(F32) - 0.001 * full).astype(BF16)
        term = lax.dot_general(
            nfull[:, :, :, cut].reshape(rows, step), new_weight,
            (((1,), (1,)), ((), ())), preferred_element_type=F32,
        )
        if n == 0:
            part[...] = term
        else:
            part[...] += term
    put = pltpu.make_async_copy(ubuf, update, local.at[3])
    put.start()

    share = rows // nc
    rsend[...] = part[...].astype(BF16).reshape(nc, share, part.shape[1])
    for d, c in col_peers:
        go(remote(rsend.at[c], rrecv.at[d - 1], r_s.at[d], r_r.at[d], (row, c)))
    total = part[pl.ds(pl.multiple_of(col * share, share), share)]
    for d, c in col_peers:
        remote(rsend.at[c], rrecv.at[d - 1], r_s.at[d], r_r.at[d], (row, c)).wait_recv()
        total = total + rrecv[d - 1].astype(F32)
    obuf[...] = total.astype(BF16)
    put_out = pltpu.make_async_copy(obuf, out, local.at[4])
    put_out.start()

    for copy in sends:
        copy.wait_send()

    for cond, copy in guards:
        @pl.when(cond)
        def _(copy=copy):
            copy.wait_send()

    for zs, valid in handed:
        @pl.when(valid)
        def _(zs=zs):
            for e, r, c, _ in plane:
                plane_copy(zs, e, slot, (r, c)).wait_send()

    put.wait()
    put_out.wait()


def per_device(
    acts, grads, next_acts, weight, moment, second, left_bank, right_bank, left_index, right_index,
    *, nr, nc,
):
    nz = nr // 2
    tok, width = acts.shape
    gtok, bo = grads.shape
    ntok = next_acts.shape[0]
    bank, rrows, _ = right_bank.shape
    lanes = width // 2
    share = nr * ntok // nc
    dma = pltpu.SemaphoreType.DMA
    anyspace = pl.BlockSpec(memory_space=pl.ANY)
    smem = pl.BlockSpec(memory_space=pltpu.SMEM)
    return pl.pallas_call(
        functools.partial(kernel, nz, nc),
        out_shape=(
            jax.ShapeDtypeStruct(weight.shape, BF16),
            jax.ShapeDtypeStruct((share, bo), BF16),
        ),
        in_specs=[anyspace] * 8 + [smem] * 2,
        out_specs=(anyspace, anyspace),
        scratch_shapes=[
            pltpu.VMEM((nz, 2, tok, width), BF16),
            pltpu.VMEM((nc * gtok, bo), BF16),
            pltpu.VMEM((nz, 2, ntok, width), BF16),
            pltpu.VMEM(weight.shape, BF16),
            pltpu.VMEM(weight.shape, F32),
            pltpu.VMEM(weight.shape, F32),
            pltpu.VMEM(left_bank.shape, BF16),
            pltpu.VMEM((nz // 2, bank, rrows, lanes), BF16),
            pltpu.VMEM((nz // 2, 8, rrows, lanes), BF16),
            pltpu.VMEM((nz // 2, 2, 2, rrows, width), BF16),
            pltpu.VMEM((8, 128), jnp.int32),
            pltpu.VMEM((8, 8, 128), jnp.int32),
            pltpu.SMEM((8, 8, 128), jnp.int32),
            pltpu.VMEM(weight.shape, F32),
            pltpu.VMEM(weight.shape, BF16),
            pltpu.VMEM(weight.shape, BF16),
            pltpu.VMEM((nr * ntok, bo), F32),
            pltpu.VMEM((nc, share, bo), BF16),
            pltpu.VMEM((nc - 1, share, bo), BF16),
            pltpu.VMEM(weight.shape, BF16),
            pltpu.VMEM((share, bo), BF16),
            dma((10,)),
            dma((nz + 2,)), dma((nz,)), dma((nz,)), dma((nz,)),
            dma((nz + 2,)), dma((nz,)), dma((1,)), dma((1,)),
            dma((nz + 2,)), dma((nz // 2,)),
            dma((nc,)), dma((nc,)),
            dma((8,)), dma((8,)), dma((nz // 2, 8)), dma((nz // 2, 8)), dma((nz // 2,)),
            dma((nc,)), dma((nc,)),
        ],
        compiler_params=pltpu.CompilerParams(
            collective_id=0, has_side_effects=True, vmem_limit_bytes=60 * 2**20,
        ),
    )(acts, grads, next_acts, weight, moment, second, left_bank, right_bank, left_index,
      right_index)


def solution(mesh):
    nr, nc = mesh.shape["row"], mesh.shape["col"]
    return jax.shard_map(
        functools.partial(per_device, nr=nr, nc=nc),
        mesh=mesh,
        in_specs=(
            P("row", "col"), P("col", "row"), P("row", "col"), P("row", "col"),
            P("row", "col"), P("row", "col"), P(), P(None, "row", None),
            P("row", "col"), P("row", "col"),
        ),
        out_specs=(P("row", "col"), P("col", "row")),
        check_vma=False,
    )
```

```python
import functools

import jax
import jax.numpy as jnp
from jax import lax
from jax.experimental import pallas as pl
from jax.experimental.pallas import tpu as pltpu
from jax.sharding import PartitionSpec as P

F32 = jnp.float32
BF16 = jnp.bfloat16
MESH = pl.DeviceIdType.MESH


def flip(value, bits, size):
    out, place = 0, 1
    while place < size:
        bit = (value // place) % 2
        out = out + place * ((1 - bit) if (bits // place) % 2 else bit)
        place *= 2
    return out


def as_matrix(value):
    cols = value.shape[-1]
    if value.shape[-2] % 16:
        return value.astype(F32).reshape(-1, cols).astype(BF16)
    return value.reshape(-1, cols)


def kernel(
    nz, nc,
    acts, grads, nxt, weight, moment, second, left_bank, right_bank, left_index, right_index,
    update, out,
    afull, gfull, nfull, wbuf, mbuf, sbuf, lbuf, bz, sel, rbuf,
    my_pick, picks, picks_smem, gacc, half, back, part, rsend, rrecv, ubuf, obuf,
    local, a_s, a_r, ay_s, ay_r, n_s, n_r, ny_s, ny_r, b_s, b_r,
    g_s, g_r, p_s, p_r, s_s, s_r, own_s, r_s, r_r,
):
    row, col = lax.axis_index("row"), lax.axis_index("col")
    z, y = row // 2, row % 2
    quad, q = col // 4, col % 4
    x, k = q // 2, q % 2
    tok = acts.shape[0]
    gtok = grads.shape[0]
    width = acts.shape[1]
    lanes = width // 2
    slot = y * 4 + q
    my_lanes = pl.ds(pl.multiple_of(x * lanes, 128), lanes)

    def remote(src, dst, ss, rs, device):
        return pltpu.make_async_remote_copy(
            src_ref=src, dst_ref=dst, send_sem=ss, recv_sem=rs,
            device_id=device, device_id_type=MESH,
        )

    z_peers = [(d, flip(z, d, nz)) for d in range(1, nz)]
    plane = [
        (dy * 4 + dq, 2 * z + ((1 - y) if dy else y), quad * 4 + flip(q, dq, 4),
         ((1 - y) if dy else y) * 4 + flip(q, dq, 4))
        for dy in range(2) for dq in range(4) if dy or dq
    ]
    col_peers = [(d, flip(col, d, nc)) for d in range(1, nc)]
    far_cols = [peer for d, peer in col_peers if d >= 4]
    mate = (2 * z + 1 - y, col)

    my_pick[...] = jnp.full(my_pick.shape, right_index[0, 0], jnp.int32)

    loads = [
        (acts, afull.at[z, y]), (nxt, nfull.at[z, y]),
        (grads, gfull.at[pl.ds(pl.multiple_of(col * gtok, gtok), gtok)]),
        (weight, wbuf), (moment, mbuf), (second, sbuf), (left_bank, lbuf),
    ]
    loads = [pltpu.make_async_copy(s, d, local.at[i]) for i, (s, d) in enumerate(loads)]
    own_bank = pltpu.make_async_copy(
        right_bank.at[:, :, my_lanes], bz.at[z // 2], local.at[7]
    )

    @pl.when(z % 2 == k)
    def _():
        own_bank.start()

    for load in loads:
        load.start()

    barrier = pltpu.get_barrier_semaphore()
    friends = [(2 * p + y, col) for _, p in z_peers]
    friends += [(r, c) for _, r, c, _ in plane]
    friends += [(row, c) for c in far_cols]
    for friend in friends:
        pl.semaphore_signal(barrier, inc=1, device_id=friend, device_id_type=MESH)
    pl.semaphore_wait(barrier, len(friends))

    sends, guards, handed = [], [], []

    def go(copy):
        copy.start()
        sends.append(copy)

    for e, r, c, _ in plane:
        go(remote(my_pick, picks.at[slot], p_s.at[e], p_r.at[slot], (r, c)))
    bank_src = right_bank.at[:, :, my_lanes]
    up, down = (2 * (z + 1) + y, col), (2 * (z - 1) + y, col)
    has_up, has_down = z < nz - 1, z > 0

    def guarded(cond, copy):
        @pl.when(cond)
        def _():
            copy.start()

        guards.append((cond, copy))

    def bank_copy(src, zs, ss, device):
        return remote(src, bz.at[zs // 2], ss, b_r.at[zs // 2], device)

    def both_ways(make, mine):
        guarded(has_up & mine, make(0, up))
        guarded(has_down & mine, make(1, down))

    yes = z >= 0
    go(remote(nxt, nfull.at[z, y], ny_s.at[0], ny_r.at[0], mate))
    both_ways(lambda i, to: bank_copy(bank_src, z, b_s.at[nz + i], to), z % 2 == k)
    both_ways(lambda i, to: remote(acts, afull.at[z, y], a_s.at[nz + i], a_r.at[z], to), yes)
    go(remote(acts, afull.at[z, y], ay_s.at[z], ay_r.at[z], mate))
    for d, c in col_peers:
        go(remote(grads, gfull.at[pl.ds(pl.multiple_of(col * gtok, gtok), gtok)],
                  g_s.at[d], g_r.at[col], (row, c)))
    loads[1].wait()
    remote(nxt, nfull.at[z, 1 - y], ny_s.at[0], ny_r.at[0], mate).wait_recv()
    both_ways(lambda i, to: remote(nfull.at[z], nfull.at[z], n_s.at[nz + i], n_r.at[z], to), yes)

    picks[slot] = my_pick[...]
    for e, r, c, s in plane:
        remote(my_pick, picks.at[s], p_s.at[e], p_r.at[s], (r, c)).wait_recv()
    to_smem = pltpu.make_async_copy(picks, picks_smem, local.at[8])
    to_smem.start()
    to_smem.wait()

    def place(zs, slot_from):
        ys, qs = slot_from // 4, slot_from % 4
        at = pl.ds(pl.multiple_of((qs // 2) * lanes, 128), lanes)
        return rbuf.at[zs // 2, qs % 2, ys, :, at]

    def plane_copy(zs, e, s, device):
        i = zs // 2
        return remote(sel.at[i, e], place(zs, s), s_s.at[i, e], s_r.at[i, s], device)

    def own_copy(zs):
        return pltpu.make_async_copy(sel.at[zs // 2, 0], place(zs, slot), own_s.at[zs // 2])

    def hand_out(zs, valid):
        @pl.when(valid)
        def _():
            for e, s in [(0, slot)] + [(e, s) for e, _, _, s in plane]:
                pick = picks_smem[s, 0, 0]
                piece = bz[zs // 2, 0]
                for b in range(1, bz.shape[1]):
                    piece = jnp.where(pick == b, bz[zs // 2, b], piece)
                sel[zs // 2, e] = piece
            own_copy(zs).start()
            for e, r, c, _ in plane:
                plane_copy(zs, e, slot, (r, c)).start()

        handed.append((zs, valid))

    @pl.when(z % 2 == k)
    def _():
        own_bank.wait()

    hand_out(z, z % 2 == k)

    def take(valid, copy):
        @pl.when(valid)
        def _():
            copy.wait_recv()

    def forward(hop, what):
        for zs, valid, on, to in ((z - hop, z >= hop, has_up, up),
                                  (z + hop, z + hop < nz, has_down, down)):
            zs = lax.rem(zs + nz, nz)
            if what == "bank":
                valid = valid & (zs % 2 == k)
                copy = bank_copy(bz.at[zs // 2], zs, b_s.at[zs], to)
            elif what == "acts":
                copy = remote(afull.at[zs, y], afull.at[zs, y], a_s.at[zs], a_r.at[zs], to)
            else:
                copy = remote(nfull.at[zs], nfull.at[zs], n_s.at[zs], n_r.at[zs], to)
            take(valid, copy)
            if hop < nz - 1:
                guarded(valid & on, copy)
            if what == "bank":
                hand_out(zs, valid)
            if what == "acts":
                guarded(valid, remote(afull.at[zs, y], afull.at[zs, y], ay_s.at[zs],
                                      ay_r.at[zs], mate))

    for hop in range(1, nz):
        forward(hop, "bank")
        if hop < nz - 1:
            forward(hop, "acts")
    forward(nz - 1, "acts")
    for hop in range(1, nz):
        forward(hop, "next")

    for i in (0, 2):
        loads[i].wait()
    for d, c in col_peers:
        remote(grads, gfull.at[pl.ds(pl.multiple_of(c * gtok, gtok), gtok)],
               g_s.at[d], g_r.at[c], (row, c)).wait_recv()

    for d in range(nz):
        zs = flip(z, d, nz) if d else z
        remote(acts, afull.at[zs, 1 - y], ay_s.at[0], ay_r.at[zs], mate).wait_recv()
        term = lax.dot_general(
            gfull[pl.ds(pl.multiple_of(zs * 2 * tok, 2 * tok), 2 * tok)],
            afull[zs].reshape(2 * tok, width),
            (((0,), (0,)), ((), ())), preferred_element_type=F32,
        )
        if d == 0:
            gacc[...] = term
        else:
            gacc[...] += term

    loads[6].wait()
    left = lbuf[left_index[0, 0]]
    half[...] = lax.dot_general(
        left, gacc[...].astype(BF16), (((0,), (0,)), ((), ())), preferred_element_type=F32
    ).astype(BF16)

    for i in range(nz // 2):
        for e, r, c, s in plane:
            plane_copy(2 * i, e, s, (r, c)).wait_recv()
    for zs, valid in handed:
        @pl.when(valid)
        def _(zs=zs):
            own_copy(zs).wait()

    for i in (3, 4, 5):
        loads[i].wait()
    step = 256 if width % 256 == 0 else width
    right = as_matrix(rbuf[...])
    for n in range(0, width, step):
        cut = slice(n, n + step)
        rotated = jnp.dot(half[...], right[:, cut], preferred_element_type=F32)
        new_moment = 0.8 * mbuf[:, cut] + 0.2 * rotated
        new_second = 0.9 * sbuf[:, cut] + 0.1 * rotated * rotated
        scaled = (new_moment / (jnp.sqrt(new_second) + 1e-08)).astype(BF16)
        back[:, cut] = jnp.dot(left, scaled, preferred_element_type=F32).astype(BF16)

    rows = nfull.shape[0] * nfull.shape[1] * nfull.shape[2]
    for n in range(0, width, step):
        cut = slice(n, n + step)
        full = lax.dot_general(
            back[...], right[cut, :], (((1,), (1,)), ((), ())), preferred_element_type=F32
        )
        ubuf[:, cut] = full.astype(BF16)
        half[:, cut] = (wbuf[:, cut].astype(F32) - 0.001 * full).astype(BF16)
    put = pltpu.make_async_copy(ubuf, update, local.at[3])
    put.start()

    share = rows // nc
    hz, hc, side = nz // 2, nc // 2, col // (nc // 2)
    for turn, at in enumerate((1 - side, side)):
        term = lax.dot_general(
            nfull[pl.ds(at * hz, hz)].reshape(rows // 2, width), half[...],
            (((1,), (1,)), ((), ())), preferred_element_type=F32,
        )
        part[pl.ds(pl.multiple_of(at * (rows // 2), rows // 2), rows // 2)] = term
        rsend[pl.ds(at * hc, hc)] = term.astype(BF16).reshape(hc, share, part.shape[1])
        for d, c in col_peers:
            if (d >= hc) == (turn == 0):
                go(remote(rsend.at[c], rrecv.at[d - 1], r_s.at[d], r_r.at[d], (row, c)))
    total = part[pl.ds(pl.multiple_of(col * share, share), share)]
    for d, c in col_peers:
        remote(rsend.at[c], rrecv.at[d - 1], r_s.at[d], r_r.at[d], (row, c)).wait_recv()
        total = total + rrecv[d - 1].astype(F32)
    obuf[...] = total.astype(BF16)
    put_out = pltpu.make_async_copy(obuf, out, local.at[4])
    put_out.start()

    for copy in sends:
        copy.wait_send()

    for cond, copy in guards:
        @pl.when(cond)
        def _(copy=copy):
            copy.wait_send()

    for zs, valid in handed:
        @pl.when(valid)
        def _(zs=zs):
            for e, r, c, _ in plane:
                plane_copy(zs, e, slot, (r, c)).wait_send()

    put.wait()
    put_out.wait()


def finish(update_in, out_in, update, out, ubuf, obuf, sems):
    rows = ubuf.shape[0] // 4
    gets, puts = [], []
    for i in range(4):
        cut = pl.ds(i * rows, rows)
        gets.append(pltpu.make_async_copy(update_in.at[cut], ubuf.at[cut], sems.at[i]))
        puts.append(pltpu.make_async_copy(ubuf.at[cut], update.at[cut], sems.at[5 + i]))
    gets.append(pltpu.make_async_copy(out_in, obuf, sems.at[4]))
    puts.append(pltpu.make_async_copy(obuf, out, sems.at[9]))
    for get in gets:
        get.start()
    for get, put in zip(gets, puts):
        get.wait()
        put.start()
    for put in puts:
        put.wait()


def per_device(
    acts, grads, next_acts, weight, moment, second, left_bank, right_bank, left_index, right_index,
    *, nr, nc,
):
    nz = nr // 2
    tok, width = acts.shape
    gtok, bo = grads.shape
    ntok = next_acts.shape[0]
    bank, rrows, _ = right_bank.shape
    lanes = width // 2
    share = nr * ntok // nc
    dma = pltpu.SemaphoreType.DMA
    anyspace = pl.BlockSpec(memory_space=pl.ANY)
    smem = pl.BlockSpec(memory_space=pltpu.SMEM)
    update, out = pl.pallas_call(
        functools.partial(kernel, nz, nc),
        out_shape=(
            jax.ShapeDtypeStruct(weight.shape, BF16),
            jax.ShapeDtypeStruct((share, bo), BF16),
        ),
        in_specs=[anyspace] * 8 + [smem] * 2,
        out_specs=(anyspace, anyspace),
        scratch_shapes=[
            pltpu.VMEM((nz, 2, tok, width), BF16),
            pltpu.VMEM((nc * gtok, bo), BF16),
            pltpu.VMEM((nz, 2, ntok, width), BF16),
            pltpu.VMEM(weight.shape, BF16),
            pltpu.VMEM(weight.shape, F32),
            pltpu.VMEM(weight.shape, F32),
            pltpu.VMEM(left_bank.shape, BF16),
            pltpu.VMEM((nz // 2, bank, rrows, lanes), BF16),
            pltpu.VMEM((nz // 2, 8, rrows, lanes), BF16),
            pltpu.VMEM((nz // 2, 2, 2, rrows, width), BF16),
            pltpu.VMEM((8, 128), jnp.int32),
            pltpu.VMEM((8, 8, 128), jnp.int32),
            pltpu.SMEM((8, 8, 128), jnp.int32),
            pltpu.VMEM(weight.shape, F32),
            pltpu.VMEM(weight.shape, BF16),
            pltpu.VMEM(weight.shape, BF16),
            pltpu.VMEM((nr * ntok, bo), F32),
            pltpu.VMEM((nc, share, bo), BF16),
            pltpu.VMEM((nc - 1, share, bo), BF16),
            pltpu.VMEM(weight.shape, BF16),
            pltpu.VMEM((share, bo), BF16),
            dma((10,)),
            dma((nz + 2,)), dma((nz,)), dma((nz,)), dma((nz,)),
            dma((nz + 2,)), dma((nz,)), dma((1,)), dma((1,)),
            dma((nz + 2,)), dma((nz // 2,)),
            dma((nc,)), dma((nc,)),
            dma((8,)), dma((8,)), dma((nz // 2, 8)), dma((nz // 2, 8)), dma((nz // 2,)),
            dma((nc,)), dma((nc,)),
        ],
        compiler_params=pltpu.CompilerParams(
            collective_id=0, has_side_effects=True, vmem_limit_bytes=60 * 2**20,
        ),
    )(acts, grads, next_acts, weight, moment, second, left_bank, right_bank, left_index,
      right_index)
    return pl.pallas_call(
        finish,
        out_shape=(
            jax.ShapeDtypeStruct(weight.shape, BF16),
            jax.ShapeDtypeStruct((share, bo), BF16),
        ),
        in_specs=[anyspace] * 2,
        out_specs=(anyspace, anyspace),
        scratch_shapes=[
            pltpu.VMEM(weight.shape, BF16), pltpu.VMEM((share, bo), BF16), dma((10,)),
        ],
    )(update, out)


def solution(mesh):
    nr, nc = mesh.shape["row"], mesh.shape["col"]
    return jax.shard_map(
        functools.partial(per_device, nr=nr, nc=nc),
        mesh=mesh,
        in_specs=(
            P("row", "col"), P("col", "row"), P("row", "col"), P("row", "col"),
            P("row", "col"), P("row", "col"), P(), P(None, "row", None),
            P("row", "col"), P("row", "col"),
        ),
        out_specs=(P("row", "col"), P("col", "row")),
        check_vma=False,
    )
```
